32 devices in a mesh: groups: 2 (over y), seq: 8 (over z, x), vocab: 2 (over core).
Axes of the slice: x: 2, y: 2, z: 4, core: 2. Of those that a mesh axis runs over, the one named last changes fastest.
Arguments:
- features: bfloat16 [2, 2048, 8192], P('vocab', 'groups', 'seq'), parts along dimension 1, may hold values from -1000 to 1000
- positions: int32 [2, 2048], P('vocab', ('groups', 'seq')), parts along dimension 1, may hold values from 0 to 511, as said below
- token_ids: int32 [2, 2048], P(None, ('groups', 'seq')), parts along dimension 1, may hold values from 0 to 1023
- valid: int32 [2, 2048], P(None, ('groups', 'seq')), parts along dimension 1, may hold values 0 or 1
- teacher_logits: bfloat16 [2, 2048, 1024], P(None, ('groups', 'seq'), 'vocab'), parts along dimension 1, may hold values from -260 to 260
- in_gain: bfloat16 [8192], replicated, may hold values from 0.5 to 1.5
- final_gain: bfloat16 [8192], replicated, may hold values from 0.5 to 1.5
- w_in: bfloat16 [64, 8192], replicated, may hold values from -0.0625 to 0.0625
- w_out: bfloat16 [64, 8192], replicated, may hold values from -0.75 to 0.75
- head: bfloat16 [1024, 8192], P('vocab'), may hold values from -8 to 8
Outputs:
- grads: float32 [16384, 128], P(('groups', 'seq', 'vocab')), parts along dimension 0
- row_loss: float32 [2, 2048], P(None, ('groups', 'seq')), parts along dimension 1
The draws below stay inside these ranges and needn't reach their ends.
There are 2 independent parts, one for each index of `groups`. The reference program is written for one: setup_inputs(seed, part) draws one part's arguments, and reference() takes and returns one part's arrays. A program takes and returns all parts, laid end to end along the dimension named above; an argument that names none is the same for every part. Nothing has to cross between parts.
Inputs may be any that keep to these rules, and one draw needn't show every extreme that they name: `positions`: each stream begins a document at its first token and at every multiple of 512 tokens, and may begin others between; inside a document the position rises by one from token to token.
All inputs are finite; a program needn't handle non-finite values. No bound on the sum of `valid` on one device may be relied on, other than what follows from the above.
Results may differ from the reference program's by a relative error of at most 0.012.
Values may be sent and summed in bfloat16 or wider, within the bound.
No kernel may reach another device: no remote copies, remote signals or barrier semaphores. Data moves between devices by JAX's collectives and lax.ppermute only.
A program may use at most 128 MiB of HBM per device.

```python
import math
import jax
import jax.numpy as jnp
import numpy as np
from jax import lax

D = 8192
VOC_DEV = 512
R = 64
TOK_DEV = 128
STREAMS = 2
STREAM = 1024
VOCAB = 1024


def draw_features(key, part):
    full_shape = (STREAMS, STREAM, D)
    key_base, key_rows, key_cols = jax.random.split(key, 3)
    base_draw = jnp.clip(jax.random.normal(key_base, full_shape, jnp.float32), -6.0, 6.0)
    row_scale = jnp.exp(jax.random.uniform(key_rows, (STREAMS, STREAM, 1), jnp.float32, 0.0, math.log(10.0)))
    col_scale = jnp.exp(jax.random.uniform(key_cols, (1, 1, D), jnp.float32, 0.0, math.log(10.0)))
    return (base_draw * row_scale * col_scale).astype(jnp.bfloat16)


def draw_positions(key, part):
    index_row = jnp.arange(STREAM, dtype=jnp.int32)[None, :]
    stream_col = jnp.arange(STREAMS, dtype=jnp.int32)[:, None]
    first_document = (stream_col == 0) & (index_row < min(STREAM, 512))
    random_starts = (jax.random.randint(key, (STREAMS, STREAM), 0, 16) == 0) & jnp.logical_not(first_document)
    starts = random_starts | (index_row % 512 == 0)
    last_start = lax.cummax(jnp.where(starts, index_row, 0), axis=1)
    return (index_row - last_start).astype(jnp.int32)


def draw_teacher_logits(key, part):
    full_shape = (STREAMS, STREAM, VOCAB)
    key_list = jax.random.split(key, 1)
    base_draw = 3.0 * jnp.clip(jax.random.normal(key_list[0], full_shape, jnp.float32), -5.0, 5.0)
    return base_draw.astype(jnp.bfloat16)


def draw_head(key, part):
    key_list = jax.random.split(key, 1)
    spread = 3.0 / math.sqrt(D)
    base_draw = jnp.clip(jax.random.normal(key_list[0], (VOCAB, D), jnp.float32), -6.0, 6.0) * spread
    return jnp.clip(base_draw, -8.0, 8.0).astype(jnp.bfloat16)


def set_ends(drawn, own_key, low, high):
    spot = [jax.random.randint(jax.random.fold_in(own_key, axis), (), 0, length) for axis, length in enumerate(drawn.shape)]
    longest = drawn.shape.index(max(drawn.shape))
    beside = spot[:longest] + [(spot[longest] + 1) % drawn.shape[longest]] + spot[longest + 1:]
    return drawn.at[tuple(spot)].set(low).at[tuple(beside)].set(high)


def rank_table(number_of, skew):
    portions = [(1 << 20) // math.isqrt(grade ** skew) + 1 for grade in range(1, number_of + 1)]
    scale = 1 + sum(portions) // (1 << 30)
    return np.cumsum(np.array([max(1, weight // scale) for weight in portions]))


def ranked(own_key, shape, count, lean):
    listing = rank_table(count, lean)
    lot = jax.random.randint(jax.random.fold_in(own_key, 1), shape, 0, int(listing[count - 1]))
    grade = jnp.searchsorted(jnp.asarray(listing, jnp.int32), lot, side="right")
    return jax.random.permutation(jax.random.fold_in(own_key, 2), count)[grade].astype(jnp.int32)


def bell_draw(rng, dims, width, most, held_as=jnp.bfloat16):
    return jnp.clip(width * jax.random.normal(rng, dims, jnp.float32), -most, most).astype(held_as)


def setup_inputs(seed: int = 0, part: int = 0) -> dict:
    arg_keys = jax.random.split(jax.random.key(seed), 11)
    part_splits = jax.random.split(jax.random.fold_in(arg_keys[10], part), 11)
    return {
        "features": draw_features(jax.random.fold_in(jax.random.fold_in(arg_keys[10], part), 71), part),
        "positions": draw_positions(jax.random.fold_in(jax.random.fold_in(arg_keys[10], part), 71), part),
        "token_ids": set_ends(ranked(part_splits[2], (STREAMS, STREAM), VOCAB, 2), jax.random.fold_in(part_splits[2], 3), 0, VOCAB - 1).astype(jnp.int32),
        "valid": set_ends((jax.random.randint(part_splits[3], (STREAMS, STREAM), 0, 4) < 3).astype(jnp.int32), jax.random.fold_in(part_splits[3], 1), 0, 1),
        "teacher_logits": draw_teacher_logits(jax.random.fold_in(jax.random.fold_in(arg_keys[10], part), 71), part),
        "in_gain": jnp.clip(1.0 + 0.1 * jax.random.normal(arg_keys[5], (D,), jnp.float32), 0.5, 1.5).astype(jnp.bfloat16),
        "final_gain": jnp.clip(1.0 + 0.1 * jax.random.normal(arg_keys[6], (D,), jnp.float32), 0.5, 1.5).astype(jnp.bfloat16),
        "w_in": bell_draw(arg_keys[7], (R, D), D ** -0.5, 0.0625),
        "w_out": bell_draw(arg_keys[8], (R, D), R ** -0.5, 0.75),
        "head": draw_head(jax.random.fold_in(arg_keys[10], 71), part),
    }


EPSILON = 1e-05
HARD_WEIGHT = 0.5
ROPE_BASE = 10000.0

def rotation(positions, halfway):
    freqs = jnp.exp(-math.log(ROPE_BASE) * jnp.arange(halfway, dtype=jnp.float32) / halfway)
    angles = positions.astype(jnp.float32)[:, None] * freqs[None, :]
    return (jnp.cos(angles), jnp.sin(angles))

def reference(features, positions, token_ids, valid, teacher_logits, in_gain, final_gain, w_in, w_out, head):
    halfway = R // 2
    slice_count = VOCAB // VOC_DEV

    def block_step(carry, inputs):
        states, places, labels, flags, teacher_raw = inputs
        values = states.astype(jnp.float32)
        inverse_in = lax.rsqrt(lax.optimization_barrier(jnp.mean(values * values, axis=-1, keepdims=True)) + EPSILON)
        normed = (values * inverse_in * in_gain.astype(jnp.float32)).astype(jnp.bfloat16)
        latent = jnp.dot(normed, w_in.T, preferred_element_type=jnp.float32)
        cosine, sine_part = rotation(places, halfway)
        leading, trailing = (latent[:, :halfway], latent[:, halfway:])
        turned = jnp.concatenate([leading * cosine - trailing * sine_part, leading * sine_part + trailing * cosine], axis=1)
        active = jax.nn.silu(turned).astype(jnp.bfloat16)
        hidden = normed.astype(jnp.float32) + jnp.dot(active, w_out, preferred_element_type=jnp.float32)
        inverse_out = lax.rsqrt(lax.optimization_barrier(jnp.mean(hidden * hidden, axis=-1, keepdims=True)) + EPSILON)
        unit_rows = hidden * inverse_out
        out_gain = final_gain.astype(jnp.float32)
        final_norm = (unit_rows * out_gain).astype(jnp.bfloat16)
        logits = jnp.dot(final_norm, head.T, preferred_element_type=jnp.float32)
        teacher = teacher_raw.astype(jnp.float32)
        student_top = lax.optimization_barrier(jnp.max(logits, axis=-1, keepdims=True))
        student_lse = student_top + jnp.log(lax.optimization_barrier(jnp.sum(jnp.exp(logits - student_top), axis=-1, keepdims=True)))
        teacher_top = lax.optimization_barrier(jnp.max(teacher, axis=-1, keepdims=True))
        teacher_lse = teacher_top + jnp.log(lax.optimization_barrier(jnp.sum(jnp.exp(teacher - teacher_top), axis=-1, keepdims=True)))
        prob_teacher = jnp.exp(teacher - teacher_lse)
        prob_student = jnp.exp(logits - student_lse)
        label_hits = labels[:, None] == jnp.arange(VOCAB, dtype=jnp.int32)[None, :]
        picked = lax.optimization_barrier(jnp.sum(jnp.where(label_hits, logits, 0.0), axis=-1))
        row_mask = flags.astype(jnp.float32)
        cross_term = lax.optimization_barrier(jnp.sum(prob_teacher * (teacher - logits), axis=-1))
        losses = row_mask * (cross_term - teacher_lse[:, 0] + student_lse[:, 0] + HARD_WEIGHT * (student_lse[:, 0] - picked))
        grad_logits = (row_mask[:, None] * (prob_student - prob_teacher + HARD_WEIGHT * (prob_student - label_hits.astype(jnp.float32)))).astype(jnp.bfloat16)
        grad_final = jnp.zeros(hidden.shape, jnp.float32)
        for slot_index in range(slice_count):
            lower_edge = slot_index * VOC_DEV
            partial_value = jnp.dot(grad_logits[:, lower_edge:lower_edge + VOC_DEV], head[lower_edge:lower_edge + VOC_DEV], preferred_element_type=jnp.float32)
            grad_final = grad_final + lax.optimization_barrier(partial_value.astype(jnp.bfloat16)).astype(jnp.float32)
        weighted = grad_final * out_gain
        grad_hidden = (inverse_out * (weighted - unit_rows * lax.optimization_barrier(jnp.mean(unit_rows * weighted, axis=-1, keepdims=True)))).astype(jnp.bfloat16)
        grad_active = jnp.dot(grad_hidden, w_out.T, preferred_element_type=jnp.float32)
        sigmoid_value = jax.nn.sigmoid(turned)
        grad_turned = grad_active * sigmoid_value * (1.0 + turned * (1.0 - sigmoid_value))
        lead_grad, trail_grad = (grad_turned[:, :halfway], grad_turned[:, halfway:])
        grad_latent = jnp.concatenate([lead_grad * cosine + trail_grad * sine_part, trail_grad * cosine - lead_grad * sine_part], axis=1).astype(jnp.bfloat16)
        into_grad = jnp.dot(normed.T, grad_latent, preferred_element_type=jnp.float32)
        outof_grad = jnp.dot(grad_hidden.T, active, preferred_element_type=jnp.float32)
        return (carry + jnp.concatenate([into_grad, outof_grad], axis=1), losses)
    inputs = (features.reshape(-1, TOK_DEV, D), positions.reshape(-1, TOK_DEV), token_ids.reshape(-1, TOK_DEV), valid.reshape(-1, TOK_DEV), teacher_logits.reshape(-1, TOK_DEV, VOCAB))
    start_value = jnp.zeros((D, 2 * R), jnp.float32)
    grad_table, losses = lax.scan(block_step, start_value, inputs)
    return (grad_table, losses.reshape(STREAMS, STREAM))
```

```python
import functools
import math

import jax
import jax.numpy as jnp
from jax import lax
from jax.experimental import pallas as pl
from jax.experimental.pallas import tpu as pltpu
from jax.sharding import PartitionSpec as P

EPSILON = 1e-05
HARD_WEIGHT = 0.5
ROPE_BASE = 10000.0
LANES = 128
F32 = jnp.float32
BF16 = jnp.bfloat16
PAIR = [(0, 1), (1, 0)]


def mirrored(place, bits):
    out = 0
    for bit in range(bits):
        out = out | (((place >> bit) & 1) << (bits - 1 - bit))
    return out


def swap_with(value, bit, count):
    return lax.ppermute(value, "seq", [(i, i ^ bit) for i in range(count)])


def swap_cores(value):
    return lax.ppermute(value, "vocab", PAIR)


def mm(lhs, rhs, lhs_dim, rhs_dim):
    return lax.dot_general(
        lhs, rhs, (((lhs_dim,), (rhs_dim,)), ((), ())), preferred_element_type=F32
    )


def partial_kernel(bits, block, pieces, index_ref, x_ref, gain_ref, *refs):
    tables, (send_ref, keep_ref, scaled_ref) = refs[:-3], refs[-3:]
    row = 0
    for table_ref, (first, count, gain_row) in zip(tables, pieces):
        scaled_ref[row : row + count, :] = (
            table_ref[first : first + count, :].astype(F32) * gain_ref[gain_row : gain_row + 1, :]
        ).astype(BF16)
        row += count
    half = 1 << (bits - 1)
    group = min(4, half)
    for base, out_ref in ((half, send_ref), (0, keep_ref)):

        def body(step, carry, base=base, out_ref=out_ref):
            rows = []
            for offset in range(group):
                owner = mirrored(base + step * group + offset, bits) ^ index_ref[0]
                rows.append(x_ref[pl.ds(pl.multiple_of(owner * block, block), block), :])
            product = mm(jnp.concatenate(rows, axis=0), scaled_ref[...], 1, 1)
            out_ref[pl.ds(step * group, group)] = product.reshape(
                group, block, product.shape[1]
            ).astype(out_ref.dtype)
            return carry

        if half == group:
            body(0, 0)
        else:
            lax.fori_loop(0, half // group, body, 0)


def partial_products(index, x, gains, tables, pieces, count, block):
    bits = count.bit_length() - 1
    width = sum(piece[1] for piece in pieces)
    columns = x.shape[1]
    local = pl.BlockSpec((x.shape[0], columns), lambda i, at: (0, 0))

    def table_spec(table):
        if table.shape[1] == columns:
            return pl.BlockSpec(table.shape, lambda i, at: (0, 0))
        return pl.BlockSpec((table.shape[0], columns), lambda i, at: (0, at[0]))

    half = count // 2
    shape = (half, block, width)
    return pl.pallas_call(
        functools.partial(partial_kernel, bits, block, pieces),
        grid_spec=pltpu.PrefetchScalarGridSpec(
            num_scalar_prefetch=1,
            grid=(1,),
            in_specs=[local, pl.BlockSpec((8, columns), lambda i, at: (0, at[0]))]
            + [table_spec(table) for table in tables],
            out_specs=[pl.BlockSpec(shape, lambda i, at: (0, 0, 0))] * 2,
            scratch_shapes=[pltpu.VMEM((width, columns), BF16)],
        ),
        out_shape=[jax.ShapeDtypeStruct(shape, BF16), jax.ShapeDtypeStruct(shape, F32)],
        cost_estimate=pl.CostEstimate(
            flops=2 * x.shape[0] * columns * width,
            bytes_accessed=2 * x.shape[0] * columns + 2 * width * columns + 6 * half * block * width,
            transcendentals=0,
        ),
        name="partial",
    )(index, x, gains, *tables)


def owner_kernel(depth, chunks, *refs):
    keeps, gots = refs[:chunks], refs[chunks : 2 * chunks]
    stats_ref, marks_ref, turn_ref, own_t_ref, far_t_ref, own_h_ref, far_h_ref, gram_ref = refs[
        2 * chunks : 2 * chunks + 8
    ]
    loss_ref, factor_ref, table_ref, table_send_ref = refs[2 * chunks + 8 :]
    sums = [keep[0] + got[0].astype(F32) for keep, got in zip(keeps, gots)]
    rank2 = LANES
    rank = rank2 // 2
    half = rank // 2
    raw_latent = sums[0][:, :rank]
    raw_cross = sums[0][:, rank:rank2]
    raw_logits = jnp.concatenate([sums[0][:, rank2:]] + sums[1:], axis=1)
    inverse_in = lax.rsqrt(stats_ref[:, 0:1] * (1.0 / depth) + EPSILON)
    latent = raw_latent * inverse_in
    cosine = turn_ref[:, :rank]
    sine = turn_ref[:, rank:rank2]

    def swapped(value):
        return jnp.concatenate([value[:, half:], value[:, :half]], axis=1)

    turned = latent * cosine + swapped(latent) * sine
    sigmoid = 1.0 / (1.0 + jnp.exp(-turned))
    active = (turned * sigmoid).astype(BF16)
    active_wide = active.astype(F32)
    gram_part = mm(active, gram_ref[...].astype(BF16), 1, 0)
    cross = raw_cross * inverse_in
    square = (
        inverse_in * inverse_in * stats_ref[:, 1:2]
        + jnp.sum(active_wide * (2.0 * cross + gram_part), axis=1, keepdims=True)
    )
    inverse_out = lax.rsqrt(jnp.maximum(square, 0.0) * (1.0 / depth) + EPSILON)
    head_out = jnp.concatenate([own_h_ref[...], far_h_ref[...]], axis=1)
    head_high = head_out.astype(BF16)
    head_low = (head_out - head_high.astype(F32)).astype(BF16)
    logits = inverse_out * (
        raw_logits * inverse_in + (mm(active, head_high, 1, 0) + mm(active, head_low, 1, 0))
    )
    teacher = jnp.concatenate([own_t_ref[...], far_t_ref[...]], axis=1).astype(F32)
    student_top = jnp.max(logits, axis=1, keepdims=True)
    student = jnp.exp(logits - student_top)
    student_total = jnp.sum(student, axis=1, keepdims=True)
    student_lse = student_top + jnp.log(student_total)
    teacher_top = jnp.max(teacher, axis=1, keepdims=True)
    weight = jnp.exp(teacher - teacher_top)
    teacher_total = jnp.sum(weight, axis=1, keepdims=True)
    teacher_lse = teacher_top + jnp.log(teacher_total)
    prob_teacher = weight * (1.0 / teacher_total)
    prob_student = student * (1.0 / student_total)
    hits = lax.broadcasted_iota(jnp.int32, logits.shape, 1) == marks_ref[:, 0:1]
    picked = jnp.sum(jnp.where(hits, logits, 0.0), axis=1, keepdims=True)
    mask = marks_ref[:, 1:2].astype(F32)
    overlap = jnp.sum(prob_teacher * (teacher - logits), axis=1, keepdims=True)
    loss_ref[...] = mask * (
        overlap - teacher_lse + student_lse + HARD_WEIGHT * (student_lse - picked)
    )
    grad_logits = (
        mask
        * (
            prob_student
            - prob_teacher
            + HARD_WEIGHT * (prob_student - jnp.where(hits, 1.0, 0.0))
        )
    ).astype(BF16)
    mean = jnp.sum(grad_logits.astype(F32) * logits, axis=1, keepdims=True) * (1.0 / depth)
    through = mm(grad_logits, head_high, 1, 1) + mm(grad_logits, head_low, 1, 1)
    grad_active = inverse_out * (through - mean * inverse_out * (cross + gram_part))
    grad_turned = grad_active * sigmoid * (1.0 + turned * (1.0 - sigmoid))
    grad_latent = grad_turned * cosine - swapped(grad_turned) * sine
    weight_back = -inverse_out * inverse_out * mean
    factor_ref[...] = jnp.concatenate(
        [inverse_in * grad_latent, (inverse_in * weight_back) * active_wide], axis=1
    ).astype(BF16)
    table = mm((inverse_out * active_wide).astype(BF16), grad_logits, 0, 0)
    slice_width = own_h_ref.shape[1]
    parts = slice_width // LANES
    for part in range(parts):
        table_ref[part * rank : (part + 1) * rank, :] = table[:, part * LANES : (part + 1) * LANES]
        table_send_ref[part * rank : (part + 1) * rank, :] = table[
            :, slice_width + part * LANES : slice_width + (part + 1) * LANES
        ].astype(BF16)
    own_gram = mm((weight_back * active_wide).astype(BF16), active, 0, 0)
    table_ref[parts * rank :, :] = jnp.concatenate([own_gram, jnp.zeros_like(own_gram)], axis=1)


def owner_step(depth, rank, keeps, gots, stats, marks, turn, teachers, heads, gram):
    block = stats.shape[0]
    slice_width = heads[0].shape[1]
    parts = slice_width // LANES
    spec = pl.BlockSpec(memory_space=pltpu.VMEM)
    operands = [*keeps, *gots, stats, marks, turn, *teachers, *heads, gram]
    return pl.pallas_call(
        functools.partial(owner_kernel, depth, len(keeps)),
        in_specs=[spec] * len(operands),
        out_specs=[spec] * 4,
        out_shape=[
            jax.ShapeDtypeStruct((block, 1), F32),
            jax.ShapeDtypeStruct((block, 2 * rank), BF16),
            jax.ShapeDtypeStruct(((parts + 1) * rank, LANES), F32),
            jax.ShapeDtypeStruct((parts * rank, LANES), BF16),
        ],
        name="owner",
    )(*operands)


def final_kernel(bits, block, rank, index_ref, x_ref, gain_ref, head_ref, out_w_ref, factor_ref,
                 table_ref, out_ref, order_ref):
    count = 1 << bits

    def body(place, carry):
        owner = mirrored(place, bits) ^ index_ref[0]
        order_ref[pl.ds(pl.multiple_of(owner * block, block), block), :] = factor_ref[
            pl.ds(pl.multiple_of(place * block, block), block), :
        ]
        return carry

    if count <= 8:
        for place in range(count):
            body(place, 0)
    else:
        lax.fori_loop(0, count, body, 0)
    slice_width = head_ref.shape[0]
    parts = slice_width // LANES
    from_x = mm(order_ref[...], x_ref[...], 0, 0) * gain_ref[1:2, :]
    table = jnp.concatenate(
        [table_ref[part * rank : (part + 1) * rank, :] for part in range(parts)], axis=1
    ).astype(BF16)
    from_head = mm(table, head_ref[...], 1, 0) * gain_ref[2:3, :]
    gram = table_ref[parts * rank :, :][:, :rank].astype(BF16)
    from_out = mm(gram, out_w_ref[...], 1, 0)
    total = jnp.concatenate([from_x[:rank], from_x[rank:] + from_head + from_out], axis=0)
    out_ref[...] = total.T


def final_step(index, x, gains, head, out_w, factor, table, count, block, pieces):
    bits = count.bit_length() - 1
    columns = x.shape[1] // pieces
    rank = out_w.shape[0]
    at_wide = lambda i, at: (0, at[0] * pieces + at[1])
    whole = lambda i, at: (0, 0)
    return pl.pallas_call(
        functools.partial(final_kernel, bits, block, rank),
        grid_spec=pltpu.PrefetchScalarGridSpec(
            num_scalar_prefetch=1,
            grid=(1,),
            in_specs=[
                pl.BlockSpec((x.shape[0], columns), lambda i, at: (0, at[1])),
                pl.BlockSpec((8, columns), at_wide),
                pl.BlockSpec((head.shape[0], columns), at_wide),
                pl.BlockSpec((rank, columns), at_wide),
                pl.BlockSpec(factor.shape, whole),
                pl.BlockSpec(table.shape, whole),
            ],
            out_specs=pl.BlockSpec((columns, 2 * rank), whole),
            scratch_shapes=[pltpu.VMEM(factor.shape, BF16)],
        ),
        out_shape=jax.ShapeDtypeStruct((columns, 2 * rank), F32),
        cost_estimate=pl.CostEstimate(
            flops=2 * x.shape[0] * columns * 2 * rank,
            bytes_accessed=2 * x.shape[0] * columns,
            transcendentals=0,
        ),
        name="final",
    )(index, x, gains, head, out_w, factor, table)


def on_device(
    features, positions, token_ids, valid, teacher_logits, in_gain, final_gain, w_in, w_out, head
):
    count = lax.axis_size("seq")
    bits = count.bit_length() - 1
    here = lax.axis_index("seq")
    core = lax.axis_index("vocab")
    x = features[0]
    block = x.shape[0] // count
    columns = x.shape[1]
    rank, depth = w_in.shape
    half = rank // 2
    slice_width = head.shape[0]
    vocabulary = 2 * slice_width

    far_head = swap_cores(lax.dynamic_slice_in_dim(head, here * columns, columns, axis=1))
    own_teacher = lax.dynamic_index_in_dim(teacher_logits, core, 0, keepdims=False)
    far_teacher = swap_cores(lax.dynamic_index_in_dim(teacher_logits, 1 - core, 0, keepdims=False))

    in_wide, final_wide = in_gain.astype(F32), final_gain.astype(F32)
    gains = jnp.stack([in_wide * final_wide, in_wide, final_wide] + [jnp.zeros_like(in_wide)] * 5)
    index = jnp.stack([here, core]).astype(jnp.int32)

    first = 256
    middle = (vocabulary - first) // 2
    inside = slice_width - first
    plans = [
        ([w_in, w_out, head], [(0, rank, 1), (0, rank, 1), (0, first, 0)]),
        ([head, far_head], [(first, inside, 0), (0, middle - inside, 0)]),
        ([far_head], [(middle - inside, slice_width - (middle - inside), 0)]),
    ]
    squares = jnp.square(x.astype(F32))
    in_columns = lax.dynamic_slice_in_dim(in_wide, here * columns, columns, axis=0)
    sums = jnp.stack([jnp.sum(squares, axis=1), jnp.sum(squares * jnp.square(in_columns), axis=1)])
    order = jnp.array([mirrored(place, bits) for place in range(count)], jnp.int32) ^ here
    stats = jnp.take(sums.reshape(2, count, block), order, axis=1)

    sends, keeps = [], []
    for tables, pieces in plans:
        send, keep = partial_products(index, x, gains, tables, pieces, count, block)
        sends.append(send)
        keeps.append(keep)
    for step in range(bits):
        bit = 1 << step
        gots = [swap_with(send, bit, count) for send in sends]
        left = count >> (step + 1)
        stats = stats[:, :left] + swap_with(stats[:, left:], bit, count)
        if step == bits - 1:
            break
        total = [keep + got.astype(F32) for keep, got in zip(keeps, gots)]
        sends = [value[left // 2 :].astype(BF16) for value in total]
        keeps = [value[: left // 2] for value in total]

    scaled_out = (w_out.astype(F32) * final_wide).astype(BF16)
    own_out = mm(scaled_out, head, 1, 1)
    far_out = swap_cores(own_out)
    gram = mm(w_out, w_out, 1, 1)

    freqs = jnp.exp(-math.log(ROPE_BASE) * jnp.arange(half, dtype=F32) / half)
    angles = positions[0].astype(F32)[:, None] * freqs[None, :]
    cosine, sine = jnp.cos(angles), jnp.sin(angles)
    turn = jnp.concatenate([cosine, cosine, -sine, sine], axis=1)
    labels = lax.dynamic_index_in_dim(token_ids, core, 0, keepdims=False)
    labels = lax.rem(labels + core * slice_width, vocabulary)
    marks = jnp.stack([labels, lax.dynamic_index_in_dim(valid, core, 0, keepdims=False)], axis=1)

    loss, factor, table, table_send = owner_step(
        depth,
        rank,
        keeps,
        gots,
        stats[:, 0].T,
        marks,
        turn,
        (own_teacher, far_teacher),
        (own_out, far_out),
        gram,
    )

    own_loss = loss.reshape(1, block)
    far_loss = swap_cores(own_loss)
    row_loss = jnp.where(
        core == 0,
        jnp.concatenate([own_loss, far_loss]),
        jnp.concatenate([far_loss, own_loss]),
    )

    got = swap_cores(table_send)
    table = jnp.concatenate([table[: got.shape[0]] + got.astype(F32), table[got.shape[0] :]])
    for step in reversed(range(bits)):
        rows = factor.shape[0]
        got = swap_with(jnp.concatenate([factor, table.astype(BF16)]), 1 << step, count)
        factor = jnp.concatenate([factor, got[:rows]])
        table = table + got[rows:].astype(F32)

    finish = functools.partial(
        final_step, x=x, gains=gains, head=head, out_w=w_out, factor=factor, table=table,
        count=count, block=block,
    )
    if (columns // 2) % LANES == 0:
        away = finish(index=jnp.stack([here, 1 - core]).astype(jnp.int32), pieces=2)
        near = finish(index=index, pieces=2)
    else:
        both = finish(index=jnp.stack([here, jnp.zeros_like(here)]).astype(jnp.int32), pieces=1)
        near = lax.dynamic_slice_in_dim(both, core * (columns // 2), columns // 2, axis=0)
        away = lax.dynamic_slice_in_dim(both, (1 - core) * (columns // 2), columns // 2, axis=0)
    return (near + swap_cores(away), row_loss)


def solution(mesh):
    placed = (
        P("vocab", "groups", "seq"),
        P("vocab", ("groups", "seq")),
        P(None, ("groups", "seq")),
        P(None, ("groups", "seq")),
        P(None, ("groups", "seq"), "vocab"),
        P(),
        P(),
        P(),
        P(),
        P("vocab", None),
    )
    return jax.shard_map(
        on_device,
        mesh=mesh,
        in_specs=placed,
        out_specs=(P(("groups", "seq", "vocab"), None), P(None, ("groups", "seq"))),
        check_vma=False,
    )
```

```python
import functools
import math

import jax
import jax.numpy as jnp
from jax import lax
from jax.experimental import pallas as pl
from jax.experimental.pallas import tpu as pltpu
from jax.sharding import PartitionSpec as P

EPSILON = 1e-05
HARD_WEIGHT = 0.5
ROPE_BASE = 10000.0
LANES = 128
F32 = jnp.float32
BF16 = jnp.bfloat16
PAIR = [(0, 1), (1, 0)]
VMEM = pl.BlockSpec(memory_space=pltpu.VMEM)
ANY = pl.BlockSpec(memory_space=pl.ANY)


def mirrored(place, bits):
    out = 0
    for bit in range(bits):
        out = out | (((place >> bit) & 1) << (bits - 1 - bit))
    return out


def swap_with(value, bit, count):
    return lax.ppermute(value, "seq", [(i, i ^ bit) for i in range(count)])


def swap_cores(value):
    return lax.ppermute(value, "vocab", PAIR)


def mm(lhs, rhs, lhs_dim, rhs_dim):
    return lax.dot_general(
        lhs, rhs, (((lhs_dim,), (rhs_dim,)), ((), ())), preferred_element_type=F32
    )


def block_products(here, bits, block, chunks, x_ref, table_ref, outs):
    quarter = 1 << (bits - 2)
    if quarter <= 2:
        group, merged = quarter, ((2, 3), (0, 1))
    else:
        group, merged = 4, ((2,), (3,), (0,), (1,))
    for quarters in merged:

        def body(step, carry, quarters=quarters):
            rows = []
            for part in quarters:
                for offset in range(group):
                    owner = mirrored(part * quarter + step * group + offset, bits) ^ here
                    rows.append(x_ref[pl.ds(pl.multiple_of(owner * block, block), block), :])
            product = mm(jnp.concatenate(rows, axis=0), table_ref[...], 1, 1)
            product = product.reshape(len(quarters), group, block, product.shape[1])
            for slot, part in enumerate(quarters):
                for (first, width, flip), (send_ref, keep_ref) in zip(chunks, outs):
                    place = (part >> 1) | ((part & 1) << 1) if flip else part
                    out_ref = send_ref if place >= 2 else keep_ref
                    out_ref[pl.ds((place & 1) * quarter + step * group, group)] = product[
                        slot, :, :, first : first + width
                    ].astype(out_ref.dtype)
            return carry

        if group == quarter:
            body(0, 0)
        else:
            lax.fori_loop(0, quarter // group, body, 0)


def chunk_shapes(chunks, count, block):
    return [
        jax.ShapeDtypeStruct((count // 2, block, width), kind)
        for _, width, _ in chunks
        for kind in (BF16, F32)
    ]


def own_kernel(bits, block, chunks, x_hbm, head_hbm, in_hbm, out_hbm, gain_in_ref, gain_out_ref, *refs):
    outs, scaled_ref = refs[: 2 * len(chunks)], refs[2 * len(chunks)]
    x_ref, head_ref, small_ref, table_ref, sems = refs[2 * len(chunks) + 1 :]
    here = lax.axis_index("seq")
    columns = x_ref.shape[1]
    rank = in_hbm.shape[0]
    mine = pl.ds(pl.multiple_of(here * columns, LANES), columns)
    copies = [
        pltpu.make_async_copy(head_hbm.at[:, mine], head_ref, sems.at[0]),
        pltpu.make_async_copy(in_hbm.at[:, mine], small_ref.at[:rank], sems.at[1]),
        pltpu.make_async_copy(out_hbm.at[:, mine], small_ref.at[rank:], sems.at[2]),
        pltpu.make_async_copy(x_hbm, x_ref, sems.at[3]),
    ]
    for copy in copies:
        copy.start()
    gain_in = gain_in_ref[:, mine].astype(F32)
    gain_both = gain_in * gain_out_ref[:, mine].astype(F32)
    copies[0].wait()
    scaled_ref[...] = (head_ref[...].astype(F32) * gain_both).astype(BF16)
    table_ref[2 * rank :, :] = scaled_ref[...]
    copies[1].wait()
    copies[2].wait()
    table_ref[: 2 * rank, :] = (small_ref[...].astype(F32) * gain_in).astype(BF16)
    copies[3].wait()
    pairs = list(zip(outs[0::2], outs[1::2]))
    block_products(here, bits, block, chunks, x_ref, table_ref, pairs)


def own_products(x, head, w_in, w_out, in_row, out_row, chunks, count, block):
    bits = count.bit_length() - 1
    columns = x.shape[1]
    width = sum(chunk[1] for chunk in chunks)
    shapes = chunk_shapes(chunks, count, block)
    shapes.append(jax.ShapeDtypeStruct((head.shape[0], columns), BF16))
    return pl.pallas_call(
        functools.partial(own_kernel, bits, block, chunks),
        in_specs=[ANY] * 4 + [VMEM] * 2,
        out_specs=[VMEM] * len(shapes),
        out_shape=shapes,
        scratch_shapes=[
            pltpu.VMEM(x.shape, BF16),
            pltpu.VMEM((head.shape[0], columns), BF16),
            pltpu.VMEM((2 * w_in.shape[0], columns), BF16),
            pltpu.VMEM((width, columns), BF16),
            pltpu.SemaphoreType.DMA((4,)),
        ],
        cost_estimate=pl.CostEstimate(
            flops=2 * x.shape[0] * columns * width,
            bytes_accessed=2 * x.shape[0] * columns + 2 * width * columns,
            transcendentals=0,
        ),
        name="own_products",
    )(x, head, w_in, w_out, in_row, out_row)


def far_kernel(bits, block, chunks, x_ref, table_ref, *outs):
    pairs = list(zip(outs[0::2], outs[1::2]))
    block_products(lax.axis_index("seq"), bits, block, chunks, x_ref, table_ref, pairs)


def far_products(x, table, chunks, count, block):
    bits = count.bit_length() - 1
    shapes = chunk_shapes(chunks, count, block)
    return pl.pallas_call(
        functools.partial(far_kernel, bits, block, chunks),
        in_specs=[VMEM] * 2,
        out_specs=[VMEM] * len(shapes),
        out_shape=shapes,
        cost_estimate=pl.CostEstimate(
            flops=2 * x.shape[0] * x.shape[1] * table.shape[0],
            bytes_accessed=2 * x.shape[0] * x.shape[1] + 2 * table.shape[0] * x.shape[1],
            transcendentals=0,
        ),
        name="far_products",
    )(x, table)


def owner_kernel(depth, slots, chunks, *refs):
    keeps, gots = refs[:chunks], refs[chunks : 2 * chunks]
    stats_ref, marks_ref, turn_ref, own_t_ref, far_t_ref, own_h_ref, far_h_ref, gram_ref = refs[
        2 * chunks : 2 * chunks + 8
    ]
    factor_ref, table_ref, away_ref, gram_out_ref = refs[2 * chunks + 8 :]
    sums = [None] * chunks
    for slot, keep, got in zip(slots, keeps, gots):
        sums[slot] = keep[0] + got[0].astype(F32)
    rank2 = LANES
    rank = rank2 // 2
    half = rank // 2
    raw_latent = sums[0][:, :rank]
    raw_cross = sums[0][:, rank:rank2]
    raw_logits = jnp.concatenate([sums[0][:, rank2:]] + sums[1:], axis=1)
    inverse_in = lax.rsqrt(stats_ref[:, 0:1] * (1.0 / depth) + EPSILON)
    latent = raw_latent * inverse_in
    cosine = turn_ref[:, :rank]
    sine = turn_ref[:, rank:rank2]

    def swapped(value):
        return jnp.concatenate([value[:, half:], value[:, :half]], axis=1)

    turned = latent * cosine + swapped(latent) * sine
    sigmoid = 1.0 / (1.0 + jnp.exp(-turned))
    active = (turned * sigmoid).astype(BF16)
    active_wide = active.astype(F32)
    gram_part = mm(active, gram_ref[...].astype(BF16), 1, 0)
    cross = raw_cross * inverse_in
    square = (
        inverse_in * inverse_in * stats_ref[:, 1:2]
        + jnp.sum(active_wide * (2.0 * cross + gram_part), axis=1, keepdims=True)
    )
    inverse_out = lax.rsqrt(jnp.maximum(square, 0.0) * (1.0 / depth) + EPSILON)
    head_out = jnp.concatenate([own_h_ref[...], far_h_ref[...]], axis=1)
    head_high = head_out.astype(BF16)
    head_low = (head_out - head_high.astype(F32)).astype(BF16)
    logits = inverse_out * (
        raw_logits * inverse_in + (mm(active, head_high, 1, 0) + mm(active, head_low, 1, 0))
    )
    teacher = jnp.concatenate([own_t_ref[...], far_t_ref[...]], axis=1).astype(F32)
    student_top = jnp.max(logits, axis=1, keepdims=True)
    student = jnp.exp(logits - student_top)
    student_total = jnp.sum(student, axis=1, keepdims=True)
    student_lse = student_top + jnp.log(student_total)
    teacher_top = jnp.max(teacher, axis=1, keepdims=True)
    weight = jnp.exp(teacher - teacher_top)
    teacher_total = jnp.sum(weight, axis=1, keepdims=True)
    teacher_lse = teacher_top + jnp.log(teacher_total)
    prob_teacher = weight * (1.0 / teacher_total)
    prob_student = student * (1.0 / student_total)
    hits = lax.broadcasted_iota(jnp.int32, logits.shape, 1) == marks_ref[:, 0:1]
    picked = jnp.sum(jnp.where(hits, logits, 0.0), axis=1, keepdims=True)
    mask = marks_ref[:, 1:2].astype(F32)
    overlap = jnp.sum(prob_teacher * (teacher - logits), axis=1, keepdims=True)
    loss = mask * (overlap - teacher_lse + student_lse + HARD_WEIGHT * (student_lse - picked))
    grad_logits = (
        mask
        * (
            prob_student
            - prob_teacher
            + HARD_WEIGHT * (prob_student - jnp.where(hits, 1.0, 0.0))
        )
    ).astype(BF16)
    mean = jnp.sum(grad_logits.astype(F32) * logits, axis=1, keepdims=True) * (1.0 / depth)
    through = mm(grad_logits, head_high, 1, 1) + mm(grad_logits, head_low, 1, 1)
    grad_active = inverse_out * (through - mean * inverse_out * (cross + gram_part))
    grad_turned = grad_active * sigmoid * (1.0 + turned * (1.0 - sigmoid))
    grad_latent = grad_turned * cosine - swapped(grad_turned) * sine
    weight_back = -inverse_out * inverse_out * mean
    factor_ref[...] = jnp.concatenate(
        [inverse_in * grad_latent, (inverse_in * weight_back) * active_wide], axis=1
    ).astype(BF16)
    table = mm((inverse_out * active_wide).astype(BF16), grad_logits, 0, 0)
    slice_width = own_h_ref.shape[1]
    parts = slice_width // LANES
    for part in range(parts):
        table_ref[part * rank : (part + 1) * rank, :] = table[:, part * LANES : (part + 1) * LANES]
        away_ref[part * rank : (part + 1) * rank, :] = table[
            :, slice_width + part * LANES : slice_width + (part + 1) * LANES
        ]
    lines = jnp.broadcast_to(loss, (loss.shape[0], LANES)).T[:8]
    table_ref[parts * rank :, :] = lines
    away_ref[parts * rank :, :] = lines
    own_gram = mm((weight_back * active_wide).astype(BF16), active, 0, 0)
    gram_out_ref[...] = jnp.concatenate([own_gram[:half], own_gram[half:]], axis=1).astype(BF16)


def owner_step(depth, rank, slots, keeps, gots, stats, marks, turn, teachers, heads, gram):
    block = stats.shape[0]
    rows = heads[0].shape[1] // LANES * rank + 8
    operands = [*keeps, *gots, stats, marks, turn, *teachers, *heads, gram]
    return pl.pallas_call(
        functools.partial(owner_kernel, depth, slots, len(keeps)),
        in_specs=[VMEM] * len(operands),
        out_specs=[VMEM] * 4,
        out_shape=[
            jax.ShapeDtypeStruct((block, 2 * rank), BF16),
            jax.ShapeDtypeStruct((rows, block), F32),
            jax.ShapeDtypeStruct((rows, block), F32),
            jax.ShapeDtypeStruct((rank // 2, 2 * rank), BF16),
        ],
        name="owner",
    )(*operands)


def final_kernel(bits, block, rank, x_ref, head_hbm, out_hbm, gain_in_ref, gain_out_ref, mine_ref,
                 got_ref, out_ref, head_ref, small_ref, order_ref, sems):
    here = lax.axis_index("seq")
    columns = x_ref.shape[1]
    mine = pl.ds(pl.multiple_of(here * columns, LANES), columns)
    copies = [
        pltpu.make_async_copy(head_hbm.at[:, mine], head_ref, sems.at[0]),
        pltpu.make_async_copy(out_hbm.at[:, mine], small_ref, sems.at[1]),
    ]
    for copy in copies:
        copy.start()
    half = 1 << (bits - 1)
    for base, source in ((0, mine_ref), (half, got_ref)):

        def body(place, carry, base=base, source=source):
            owner = mirrored(base + place, bits) ^ here
            order_ref[pl.ds(pl.multiple_of(owner * block, block), block), :] = source[
                pl.ds(pl.multiple_of(place * block, block), block), :
            ]
            return carry

        if half <= 8:
            for place in range(half):
                body(place, 0)
        else:
            lax.fori_loop(0, half, body, 0)
    parts = head_ref.shape[0] // LANES
    rows = half * block
    summed = mine_ref[rows:, :].astype(F32) + got_ref[rows:, :].astype(F32)
    table = jnp.concatenate(
        [summed[part * rank : (part + 1) * rank, :] for part in range(parts)], axis=1
    ).astype(BF16)
    packed = summed[parts * rank :, :]
    gram = jnp.concatenate([packed[:, :rank], packed[:, rank:]], axis=0).astype(BF16)
    from_x = mm(order_ref[...], x_ref[...], 0, 0) * gain_in_ref[:, mine].astype(F32)
    for copy in copies:
        copy.wait()
    from_head = mm(table, head_ref[...], 1, 0) * gain_out_ref[:, mine].astype(F32)
    from_out = mm(gram, small_ref[...], 1, 0)
    total = jnp.concatenate([from_x[:rank], from_x[rank:] + from_head + from_out], axis=0)
    out_ref[...] = total.T


def final_step(x, head, w_out, in_row, out_row, mine, got, count, block):
    bits = count.bit_length() - 1
    columns = x.shape[1]
    rank = w_out.shape[0]
    return pl.pallas_call(
        functools.partial(final_kernel, bits, block, rank),
        in_specs=[VMEM, ANY, ANY, VMEM, VMEM, VMEM, VMEM],
        out_specs=VMEM,
        out_shape=jax.ShapeDtypeStruct((columns, 2 * rank), F32),
        scratch_shapes=[
            pltpu.VMEM((head.shape[0], columns), BF16),
            pltpu.VMEM((rank, columns), BF16),
            pltpu.VMEM((x.shape[0], 2 * rank), BF16),
            pltpu.SemaphoreType.DMA((2,)),
        ],
        name="final",
    )(x, head, w_out, in_row, out_row, mine, got)


def on_device(
    features, positions, token_ids, valid, teacher_logits, in_gain, final_gain, w_in, w_out, head
):
    count = lax.axis_size("seq")
    bits = count.bit_length() - 1
    here = lax.axis_index("seq")
    core = lax.axis_index("vocab")
    x = features[0]
    block = x.shape[0] // count
    columns = x.shape[1]
    rank, depth = w_in.shape
    half = rank // 2
    slice_width = head.shape[0]
    vocabulary = 2 * slice_width
    in_row, out_row = in_gain.reshape(1, depth), final_gain.reshape(1, depth)

    width = 2 * rank + slice_width
    early = [(0, width - 256, False), (width - 256, 256, True)]
    late = [(0, slice_width // 2, False), (slice_width // 2, slice_width // 2, False)]
    made = own_products(x, head, w_in, w_out, in_row, out_row, early, count, block)
    far_table = swap_cores(made[-1])
    more = far_products(x, far_table, late, count, block)
    sends = [made[0], made[2], more[0], more[2]]
    keeps = [made[1], made[3], more[1], more[3]]
    flips = [chunk[2] for chunk in early + late]

    x_late, late_args, more = lax.optimization_barrier(
        (x, (positions, token_ids, valid, teacher_logits, in_gain, final_gain, w_out, head), more)
    )
    positions, token_ids, valid, teacher_logits, in_gain, final_gain, w_late, head_late = late_args
    in_wide, final_wide = in_gain.astype(F32), final_gain.astype(F32)
    squares = jnp.square(x_late.astype(F32))
    in_columns = lax.dynamic_slice_in_dim(in_wide, here * columns, columns, axis=0)
    sums = jnp.stack([jnp.sum(squares, axis=1), jnp.sum(squares * jnp.square(in_columns), axis=1)])
    order = jnp.array([mirrored(place, bits) for place in range(count)], jnp.int32) ^ here
    stats = jnp.take(sums.reshape(2, count, block), order, axis=1)
    own_teacher = lax.dynamic_index_in_dim(teacher_logits, core, 0, keepdims=False)
    far_teacher = swap_cores(lax.dynamic_index_in_dim(teacher_logits, 1 - core, 0, keepdims=False))

    scaled_out = (w_late.astype(F32) * final_wide).astype(BF16)
    own_out = mm(scaled_out, head_late, 1, 1)
    far_out = swap_cores(own_out)
    gram = mm(w_late, w_late, 1, 1)

    freqs = jnp.exp(-math.log(ROPE_BASE) * jnp.arange(half, dtype=F32) / half)
    angles = positions[0].astype(F32)[:, None] * freqs[None, :]
    cosine, sine = jnp.cos(angles), jnp.sin(angles)
    turn = jnp.concatenate([cosine, cosine, -sine, sine], axis=1)
    labels = lax.dynamic_index_in_dim(token_ids, core, 0, keepdims=False)
    labels = lax.rem(labels + core * slice_width, vocabulary)
    marks = jnp.stack([labels, lax.dynamic_index_in_dim(valid, core, 0, keepdims=False)], axis=1)

    for step in range(bits):
        gots = [
            swap_with(send, (1 << (1 - step if flip and step < 2 else step)), count)
            for send, flip in zip(sends, flips)
        ]
        left = count >> (step + 1)
        stats = stats[:, :left] + swap_with(stats[:, left:], 1 << step, count)
        if step == bits - 1:
            break
        keeps = [keep[:left] + got.astype(F32) for keep, got in zip(keeps, gots)]
        sends = [value[left // 2 :].astype(BF16) for value in keeps]

    factor, table, away, gram_out = owner_step(
        depth, rank, (0, 1, 2, 3), keeps, gots, stats[:, 0].T, marks, turn,
        (own_teacher, far_teacher), (own_out, far_out), gram,
    )
    got = swap_cores(away)
    rows = table.shape[0] - 8
    payload = jnp.concatenate([factor, (table[:rows] + got[:rows]).astype(BF16), gram_out])
    own_loss, far_loss = table[rows : rows + 1], got[rows : rows + 1]
    row_loss = jnp.where(
        core == 0,
        jnp.concatenate([own_loss, far_loss]),
        jnp.concatenate([far_loss, own_loss]),
    )
    split = block
    for step in reversed(range(bits)):
        got = swap_with(payload, 1 << step, count)
        if step:
            added = payload[split:].astype(F32) + got[split:].astype(F32)
            payload = jnp.concatenate([payload[:split], got[:split], added.astype(BF16)])
            split *= 2
            if step == 1:
                payload, row_loss = lax.optimization_barrier((payload, row_loss))

    both = final_step(x, head, w_out, in_row, out_row, payload, got, count, block)
    near = lax.dynamic_slice_in_dim(both, core * (columns // 2), columns // 2, axis=0)
    away = lax.dynamic_slice_in_dim(both, (1 - core) * (columns // 2), columns // 2, axis=0)
    return (near + swap_cores(away), row_loss)


def solution(mesh):
    placed = (
        P("vocab", "groups", "seq"),
        P("vocab", ("groups", "seq")),
        P(None, ("groups", "seq")),
        P(None, ("groups", "seq")),
        P(None, ("groups", "seq"), "vocab"),
        P(),
        P(),
        P(),
        P(),
        P("vocab", None),
    )
    return jax.shard_map(
        on_device,
        mesh=mesh,
        in_specs=placed,
        out_specs=(P(("groups", "seq", "vocab"), None), P(None, ("groups", "seq"))),
        check_vma=False,
    )
```

```python
import functools
import math

import jax
import jax.numpy as jnp
from jax import lax
from jax.experimental import pallas as pl
from jax.experimental.pallas import tpu as pltpu
from jax.sharding import PartitionSpec as P

EPSILON = 1e-05
HARD_WEIGHT = 0.5
ROPE_BASE = 10000.0
LANES = 128
F32 = jnp.float32
BF16 = jnp.bfloat16
PAIR = [(0, 1), (1, 0)]
VMEM = pl.BlockSpec(memory_space=pltpu.VMEM)
ANY = pl.BlockSpec(memory_space=pl.ANY)


def mirrored(place, bits):
    out = 0
    for bit in range(bits):
        out = out | (((place >> bit) & 1) << (bits - 1 - bit))
    return out


def swap_with(value, bit, count):
    return lax.ppermute(value, "seq", [(i, i ^ bit) for i in range(count)])


def swap_cores(value):
    return lax.ppermute(value, "vocab", PAIR)


def mm(lhs, rhs, lhs_dim, rhs_dim):
    return lax.dot_general(
        lhs, rhs, (((lhs_dim,), (rhs_dim,)), ((), ())), preferred_element_type=F32
    )


def block_products(here, bits, block, chunks, x_ref, table_ref, outs):
    quarter = 1 << (bits - 2)
    if quarter <= 2:
        group, merged = quarter, ((2, 3), (0, 1))
    else:
        group, merged = 4, ((2,), (3,), (0,), (1,))
    for quarters in merged:

        def body(step, carry, quarters=quarters):
            rows = []
            for part in quarters:
                for offset in range(group):
                    owner = mirrored(part * quarter + step * group + offset, bits) ^ here
                    rows.append(x_ref[pl.ds(pl.multiple_of(owner * block, block), block), :])
            product = mm(jnp.concatenate(rows, axis=0), table_ref[...], 1, 1)
            product = product.reshape(len(quarters), group, block, product.shape[1])
            for slot, part in enumerate(quarters):
                for (first, width, flip), (send_ref, keep_ref) in zip(chunks, outs):
                    place = (part >> 1) | ((part & 1) << 1) if flip else part
                    out_ref = send_ref if place >= 2 else keep_ref
                    out_ref[pl.ds((place & 1) * quarter + step * group, group)] = product[
                        slot, :, :, first : first + width
                    ].astype(out_ref.dtype)
            return carry

        if group == quarter:
            body(0, 0)
        else:
            lax.fori_loop(0, quarter // group, body, 0)


def chunk_shapes(chunks, count, block):
    return [
        jax.ShapeDtypeStruct((count // 2, block, width), kind)
        for _, width, _ in chunks
        for kind in (BF16, F32)
    ]


def own_kernel(bits, block, chunks, x_hbm, head_hbm, in_hbm, out_hbm, gain_in_ref, gain_out_ref, *refs):
    outs, scaled_ref = refs[: 2 * len(chunks)], refs[2 * len(chunks)]
    x_ref, head_ref, small_ref, table_ref, sems = refs[2 * len(chunks) + 1 :]
    here = lax.axis_index("seq")
    columns = x_ref.shape[1]
    rank = in_hbm.shape[0]
    mine = pl.ds(pl.multiple_of(here * columns, LANES), columns)
    copies = [
        pltpu.make_async_copy(head_hbm.at[:, mine], head_ref, sems.at[0]),
        pltpu.make_async_copy(in_hbm.at[:, mine], small_ref.at[:rank], sems.at[1]),
        pltpu.make_async_copy(out_hbm.at[:, mine], small_ref.at[rank:], sems.at[2]),
        pltpu.make_async_copy(x_hbm, x_ref, sems.at[3]),
    ]
    for copy in copies:
        copy.start()
    gain_in = gain_in_ref[:, mine].astype(F32)
    gain_both = gain_in * gain_out_ref[:, mine].astype(F32)
    copies[0].wait()
    scaled_ref[...] = (head_ref[...].astype(F32) * gain_both).astype(BF16)
    table_ref[2 * rank :, :] = scaled_ref[...]
    copies[1].wait()
    copies[2].wait()
    table_ref[: 2 * rank, :] = (small_ref[...].astype(F32) * gain_in).astype(BF16)
    copies[3].wait()
    pairs = list(zip(outs[0::2], outs[1::2]))
    block_products(here, bits, block, chunks, x_ref, table_ref, pairs)


def own_products(x, head, w_in, w_out, in_row, out_row, chunks, count, block):
    bits = count.bit_length() - 1
    columns = x.shape[1]
    width = sum(chunk[1] for chunk in chunks)
    shapes = chunk_shapes(chunks, count, block)
    shapes.append(jax.ShapeDtypeStruct((head.shape[0], columns), BF16))
    return pl.pallas_call(
        functools.partial(own_kernel, bits, block, chunks),
        in_specs=[ANY] * 4 + [VMEM] * 2,
        out_specs=[VMEM] * len(shapes),
        out_shape=shapes,
        scratch_shapes=[
            pltpu.VMEM(x.shape, BF16),
            pltpu.VMEM((head.shape[0], columns), BF16),
            pltpu.VMEM((2 * w_in.shape[0], columns), BF16),
            pltpu.VMEM((width, columns), BF16),
            pltpu.SemaphoreType.DMA((4,)),
        ],
        cost_estimate=pl.CostEstimate(
            flops=2 * x.shape[0] * columns * width,
            bytes_accessed=2 * x.shape[0] * columns + 2 * width * columns,
            transcendentals=0,
        ),
        name="own_products",
    )(x, head, w_in, w_out, in_row, out_row)


def far_kernel(bits, block, chunks, x_ref, table_ref, *outs):
    pairs = list(zip(outs[0::2], outs[1::2]))
    block_products(lax.axis_index("seq"), bits, block, chunks, x_ref, table_ref, pairs)


def far_products(x, table, chunks, count, block):
    bits = count.bit_length() - 1
    shapes = chunk_shapes(chunks, count, block)
    return pl.pallas_call(
        functools.partial(far_kernel, bits, block, chunks),
        in_specs=[VMEM] * 2,
        out_specs=[VMEM] * len(shapes),
        out_shape=shapes,
        cost_estimate=pl.CostEstimate(
            flops=2 * x.shape[0] * x.shape[1] * table.shape[0],
            bytes_accessed=2 * x.shape[0] * x.shape[1] + 2 * table.shape[0] * x.shape[1],
            transcendentals=0,
        ),
        name="far_products",
    )(x, table)


def owner_kernel(depth, slots, chunks, *refs):
    keeps, gots = refs[:chunks], refs[chunks : 2 * chunks]
    stats_ref, marks_ref, turn_ref, own_t_ref, far_t_ref, own_h_ref, far_h_ref, gram_ref = refs[
        2 * chunks : 2 * chunks + 8
    ]
    factor_ref, table_ref, away_ref, gram_out_ref = refs[2 * chunks + 8 :]
    sums = [None] * chunks
    for slot, keep, got in zip(slots, keeps, gots):
        sums[slot] = keep[0] + got[0].astype(F32)
    rank2 = LANES
    rank = rank2 // 2
    half = rank // 2
    raw_latent = sums[0][:, :rank]
    raw_cross = sums[0][:, rank:rank2]
    raw_logits = jnp.concatenate([sums[0][:, rank2:]] + sums[1:], axis=1)
    inverse_in = lax.rsqrt(stats_ref[:, 0:1] * (1.0 / depth) + EPSILON)
    latent = raw_latent * inverse_in
    cosine = turn_ref[:, :rank]
    sine = turn_ref[:, rank:rank2]

    def swapped(value):
        return jnp.concatenate([value[:, half:], value[:, :half]], axis=1)

    turned = latent * cosine + swapped(latent) * sine
    sigmoid = 1.0 / (1.0 + jnp.exp(-turned))
    active = (turned * sigmoid).astype(BF16)
    active_wide = active.astype(F32)
    gram_part = mm(active, gram_ref[...].astype(BF16), 1, 0)
    cross = raw_cross * inverse_in
    square = (
        inverse_in * inverse_in * stats_ref[:, 1:2]
        + jnp.sum(active_wide * (2.0 * cross + gram_part), axis=1, keepdims=True)
    )
    inverse_out = lax.rsqrt(jnp.maximum(square, 0.0) * (1.0 / depth) + EPSILON)
    head_out = jnp.concatenate([own_h_ref[...], far_h_ref[...]], axis=1)
    head_high = head_out.astype(BF16)
    head_low = (head_out - head_high.astype(F32)).astype(BF16)
    logits = inverse_out * (
        raw_logits * inverse_in + (mm(active, head_high, 1, 0) + mm(active, head_low, 1, 0))
    )
    teacher = jnp.concatenate([own_t_ref[...], far_t_ref[...]], axis=1).astype(F32)
    student_top = jnp.max(logits, axis=1, keepdims=True)
    student = jnp.exp(logits - student_top)
    student_total = jnp.sum(student, axis=1, keepdims=True)
    student_lse = student_top + jnp.log(student_total)
    teacher_top = jnp.max(teacher, axis=1, keepdims=True)
    weight = jnp.exp(teacher - teacher_top)
    teacher_total = jnp.sum(weight, axis=1, keepdims=True)
    teacher_lse = teacher_top + jnp.log(teacher_total)
    prob_teacher = weight * (1.0 / teacher_total)
    prob_student = student * (1.0 / student_total)
    hits = lax.broadcasted_iota(jnp.int32, logits.shape, 1) == marks_ref[:, 0:1]
    picked = jnp.sum(jnp.where(hits, logits, 0.0), axis=1, keepdims=True)
    mask = marks_ref[:, 1:2].astype(F32)
    overlap = jnp.sum(prob_teacher * (teacher - logits), axis=1, keepdims=True)
    loss = mask * (overlap - teacher_lse + student_lse + HARD_WEIGHT * (student_lse - picked))
    grad_logits = (
        mask
        * (
            prob_student
            - prob_teacher
            + HARD_WEIGHT * (prob_student - jnp.where(hits, 1.0, 0.0))
        )
    ).astype(BF16)
    mean = jnp.sum(grad_logits.astype(F32) * logits, axis=1, keepdims=True) * (1.0 / depth)
    through = mm(grad_logits, head_high, 1, 1) + mm(grad_logits, head_low, 1, 1)
    grad_active = inverse_out * (through - mean * inverse_out * (cross + gram_part))
    grad_turned = grad_active * sigmoid * (1.0 + turned * (1.0 - sigmoid))
    grad_latent = grad_turned * cosine - swapped(grad_turned) * sine
    weight_back = -inverse_out * inverse_out * mean
    factor_ref[...] = jnp.concatenate(
        [inverse_in * grad_latent, (inverse_in * weight_back) * active_wide], axis=1
    ).astype(BF16)
    table = mm((inverse_out * active_wide).astype(BF16), grad_logits, 0, 0)
    slice_width = own_h_ref.shape[1]
    parts = slice_width // LANES
    for part in range(parts):
        table_ref[part * rank : (part + 1) * rank, :] = table[:, part * LANES : (part + 1) * LANES]
        away_ref[part * rank : (part + 1) * rank, :] = table[
            :, slice_width + part * LANES : slice_width + (part + 1) * LANES
        ]
    lines = jnp.broadcast_to(loss, (loss.shape[0], LANES)).T[:8]
    table_ref[parts * rank :, :] = lines
    away_ref[parts * rank :, :] = lines
    own_gram = mm((weight_back * active_wide).astype(BF16), active, 0, 0)
    gram_out_ref[...] = jnp.concatenate([own_gram[:half], own_gram[half:]], axis=1).astype(BF16)


def owner_step(depth, rank, slots, keeps, gots, stats, marks, turn, teachers, heads, gram):
    block = stats.shape[0]
    rows = heads[0].shape[1] // LANES * rank + 8
    operands = [*keeps, *gots, stats, marks, turn, *teachers, *heads, gram]
    return pl.pallas_call(
        functools.partial(owner_kernel, depth, slots, len(keeps)),
        in_specs=[VMEM] * len(operands),
        out_specs=[VMEM] * 4,
        out_shape=[
            jax.ShapeDtypeStruct((block, 2 * rank), BF16),
            jax.ShapeDtypeStruct((rows, block), F32),
            jax.ShapeDtypeStruct((rows, block), F32),
            jax.ShapeDtypeStruct((rank // 2, 2 * rank), BF16),
        ],
        name="owner",
    )(*operands)


def first_payload_kernel(factor_ref, table_ref, got_ref, gram_ref, out_ref):
    block = factor_ref.shape[0]
    rows = table_ref.shape[0] - 8
    out_ref[:block, :] = factor_ref[...]
    out_ref[block : block + rows, :] = (table_ref[:rows, :] + got_ref[:rows, :]).astype(BF16)
    out_ref[block + rows :, :] = gram_ref[...]


def next_payload_kernel(split, mine_ref, got_ref, out_ref):
    out_ref[:split, :] = mine_ref[:split, :]
    out_ref[split : 2 * split, :] = got_ref[:split, :]
    out_ref[2 * split :, :] = (
        mine_ref[split:, :].astype(F32) + got_ref[split:, :].astype(F32)
    ).astype(BF16)


def joined(kernel, rows, *operands):
    return pl.pallas_call(
        kernel,
        in_specs=[VMEM] * len(operands),
        out_specs=VMEM,
        out_shape=jax.ShapeDtypeStruct((rows, LANES), BF16),
        name="joined",
    )(*operands)


def final_kernel(bits, block, rank, x_ref, head_hbm, out_hbm, gain_in_ref, gain_out_ref, mine_ref,
                 got_ref, near_ref, away_ref, turned_ref, head_ref, small_ref, order_ref, sems):
    here = lax.axis_index("seq")
    columns = x_ref.shape[1]
    mine = pl.ds(pl.multiple_of(here * columns, LANES), columns)
    copies = [
        pltpu.make_async_copy(head_hbm.at[:, mine], head_ref, sems.at[0]),
        pltpu.make_async_copy(out_hbm.at[:, mine], small_ref, sems.at[1]),
    ]
    for copy in copies:
        copy.start()
    half = 1 << (bits - 1)
    for base, source in ((0, mine_ref), (half, got_ref)):

        def body(place, carry, base=base, source=source):
            owner = mirrored(base + place, bits) ^ here
            order_ref[pl.ds(pl.multiple_of(owner * block, block), block), :] = source[
                pl.ds(pl.multiple_of(place * block, block), block), :
            ]
            return carry

        if half <= 8:
            for place in range(half):
                body(place, 0)
        else:
            lax.fori_loop(0, half, body, 0)
    parts = head_ref.shape[0] // LANES
    rows = half * block
    summed = mine_ref[rows:, :].astype(F32) + got_ref[rows:, :].astype(F32)
    table = jnp.concatenate(
        [summed[part * rank : (part + 1) * rank, :] for part in range(parts)], axis=1
    ).astype(BF16)
    packed = summed[parts * rank :, :]
    gram = jnp.concatenate([packed[:, :rank], packed[:, rank:]], axis=0).astype(BF16)
    from_x = mm(order_ref[...], x_ref[...], 0, 0) * gain_in_ref[:, mine].astype(F32)
    for copy in copies:
        copy.wait()
    from_head = mm(table, head_ref[...], 1, 0) * gain_out_ref[:, mine].astype(F32)
    from_out = mm(gram, small_ref[...], 1, 0)
    total = jnp.concatenate([from_x[:rank], from_x[rank:] + from_head + from_out], axis=0)
    turned_ref[...] = total.T
    rows = columns // 2
    core = lax.axis_index("vocab")
    near_ref[...] = turned_ref[pl.ds(pl.multiple_of(core * rows, 8), rows), :]
    away_ref[...] = turned_ref[pl.ds(pl.multiple_of((1 - core) * rows, 8), rows), :]


def final_step(x, head, w_out, in_row, out_row, mine, got, count, block):
    bits = count.bit_length() - 1
    columns = x.shape[1]
    rank = w_out.shape[0]
    return pl.pallas_call(
        functools.partial(final_kernel, bits, block, rank),
        in_specs=[VMEM, ANY, ANY, VMEM, VMEM, VMEM, VMEM],
        out_specs=[VMEM] * 2,
        out_shape=[jax.ShapeDtypeStruct((columns // 2, 2 * rank), F32)] * 2,
        scratch_shapes=[
            pltpu.VMEM((columns, 2 * rank), F32),
            pltpu.VMEM((head.shape[0], columns), BF16),
            pltpu.VMEM((rank, columns), BF16),
            pltpu.VMEM((x.shape[0], 2 * rank), BF16),
            pltpu.SemaphoreType.DMA((2,)),
        ],
        name="final",
    )(x, head, w_out, in_row, out_row, mine, got)


def on_device(
    features, positions, token_ids, valid, teacher_logits, in_gain, final_gain, w_in, w_out, head
):
    count = lax.axis_size("seq")
    bits = count.bit_length() - 1
    here = lax.axis_index("seq")
    core = lax.axis_index("vocab")
    x = features[0]
    block = x.shape[0] // count
    columns = x.shape[1]
    rank, depth = w_in.shape
    half = rank // 2
    slice_width = head.shape[0]
    vocabulary = 2 * slice_width
    in_row, out_row = in_gain.reshape(1, depth), final_gain.reshape(1, depth)

    width = 2 * rank + slice_width
    early = [(0, width - 256, False), (width - 256, 256, True)]
    late = [(0, slice_width // 2, False), (slice_width // 2, slice_width // 2, False)]
    made = own_products(x, head, w_in, w_out, in_row, out_row, early, count, block)
    far_table = swap_cores(made[-1])
    more = far_products(x, far_table, late, count, block)
    sends = [made[0], made[2], more[0], more[2]]
    keeps = [made[1], made[3], more[1], more[3]]
    flips = [chunk[2] for chunk in early + late]

    x_late, late_args, more = lax.optimization_barrier(
        (x, (positions, token_ids, valid, teacher_logits, in_gain, final_gain, w_out, head), more)
    )
    positions, token_ids, valid, teacher_logits, in_gain, final_gain, w_late, head_late = late_args
    in_wide, final_wide = in_gain.astype(F32), final_gain.astype(F32)
    squares = jnp.square(x_late.astype(F32))
    in_columns = lax.dynamic_slice_in_dim(in_wide, here * columns, columns, axis=0)
    sums = jnp.stack([jnp.sum(squares, axis=1), jnp.sum(squares * jnp.square(in_columns), axis=1)])
    order = jnp.array([mirrored(place, bits) for place in range(count)], jnp.int32) ^ here
    stats = jnp.take(sums.reshape(2, count, block), order, axis=1)
    own_teacher = lax.dynamic_index_in_dim(teacher_logits, core, 0, keepdims=False)
    far_teacher = swap_cores(lax.dynamic_index_in_dim(teacher_logits, 1 - core, 0, keepdims=False))

    scaled_out = (w_late.astype(F32) * final_wide).astype(BF16)
    own_out = mm(scaled_out, head_late, 1, 1)
    far_out = swap_cores(own_out)
    gram = mm(w_late, w_late, 1, 1)

    freqs = jnp.exp(-math.log(ROPE_BASE) * jnp.arange(half, dtype=F32) / half)
    angles = positions[0].astype(F32)[:, None] * freqs[None, :]
    cosine, sine = jnp.cos(angles), jnp.sin(angles)
    turn = jnp.concatenate([cosine, cosine, -sine, sine], axis=1)
    labels = lax.dynamic_index_in_dim(token_ids, core, 0, keepdims=False)
    labels = lax.rem(labels + core * slice_width, vocabulary)
    marks = jnp.stack([labels, lax.dynamic_index_in_dim(valid, core, 0, keepdims=False)], axis=1)

    for step in range(bits):
        gots = [
            swap_with(send, (1 << (1 - step if flip and step < 2 else step)), count)
            for send, flip in zip(sends, flips)
        ]
        if step == 0:
            first_gots, _ = lax.optimization_barrier((gots[: len(early)], more[0]))
            gots = list(first_gots) + gots[len(early) :]
        left = count >> (step + 1)
        stats = stats[:, :left] + swap_with(stats[:, left:], 1 << step, count)
        if step == bits - 1:
            break
        keeps = [keep[:left] + got.astype(F32) for keep, got in zip(keeps, gots)]
        sends = [value[left // 2 :].astype(BF16) for value in keeps]

    factor, table, away, gram_out = owner_step(
        depth, rank, (0, 1, 2, 3), keeps, gots, stats[:, 0].T, marks, turn,
        (own_teacher, far_teacher), (own_out, far_out), gram,
    )
    got = swap_cores(away)
    rows = table.shape[0] - 8
    payload = joined(
        first_payload_kernel, block + rows + rank // 2, factor, table, got, gram_out
    )
    own_loss, far_loss = table[rows : rows + 1], got[rows : rows + 1]
    row_loss = jnp.where(
        core == 0,
        jnp.concatenate([own_loss, far_loss]),
        jnp.concatenate([far_loss, own_loss]),
    )
    split = block
    for step in reversed(range(bits)):
        got = swap_with(payload, 1 << step, count)
        if step:
            kernel = functools.partial(next_payload_kernel, split)
            payload = joined(kernel, payload.shape[0] + split, payload, got)
            split *= 2
            if step == 1:
                payload, row_loss = lax.optimization_barrier((payload, row_loss))

    near, away = final_step(x, head, w_out, in_row, out_row, payload, got, count, block)
    return (near + swap_cores(away), row_loss)


def solution(mesh):
    placed = (
        P("vocab", "groups", "seq"),
        P("vocab", ("groups", "seq")),
        P(None, ("groups", "seq")),
        P(None, ("groups", "seq")),
        P(None, ("groups", "seq"), "vocab"),
        P(),
        P(),
        P(),
        P(),
        P("vocab", None),
    )
    return jax.shard_map(
        on_device,
        mesh=mesh,
        in_specs=placed,
        out_specs=(P(("groups", "seq", "vocab"), None), P(None, ("groups", "seq"))),
        check_vma=False,
    )
```

```python
import functools
import math

import jax
import jax.numpy as jnp
from jax import lax
from jax.experimental import pallas as pl
from jax.experimental.pallas import tpu as pltpu
from jax.sharding import PartitionSpec as P

EPSILON = 1e-05
HARD_WEIGHT = 0.5
ROPE_BASE = 10000.0
LANES = 128
F32 = jnp.float32
BF16 = jnp.bfloat16
PAIR = [(0, 1), (1, 0)]
VMEM = pl.BlockSpec(memory_space=pltpu.VMEM)
ANY = pl.BlockSpec(memory_space=pl.ANY)


def mirrored(place, bits):
    out = 0
    for bit in range(bits):
        out = out | (((place >> bit) & 1) << (bits - 1 - bit))
    return out


def swap_with(value, bit, count):
    return lax.ppermute(value, "seq", [(i, i ^ bit) for i in range(count)])


def swap_cores(value):
    return lax.ppermute(value, "vocab", PAIR)


def mm(lhs, rhs, lhs_dim, rhs_dim):
    return lax.dot_general(
        lhs, rhs, (((lhs_dim,), (rhs_dim,)), ((), ())), preferred_element_type=F32
    )


def gain_row(gain_ref, mine):
    if len(gain_ref.shape) == 1:
        return gain_ref[mine].reshape(1, mine.size).astype(F32)
    return gain_ref[:, mine].astype(F32)


def block_products(here, bits, block, chunks, x_ref, table_ref, outs):
    quarter = 1 << (bits - 2)
    if quarter <= 2:
        group, merged = quarter, ((2, 3), (0, 1))
    else:
        group, merged = 4, ((2,), (3,), (0,), (1,))
    for quarters in merged:

        def body(step, carry, quarters=quarters):
            rows = []
            for part in quarters:
                for offset in range(group):
                    owner = mirrored(part * quarter + step * group + offset, bits) ^ here
                    rows.append(x_ref[pl.ds(pl.multiple_of(owner * block, block), block), :])
            product = mm(jnp.concatenate(rows, axis=0), table_ref[...], 1, 1)
            product = product.reshape(len(quarters), group, block, product.shape[1])
            for slot, part in enumerate(quarters):
                for (first, width, flip), (send_ref, keep_ref) in zip(chunks, outs):
                    place = (part >> 1) | ((part & 1) << 1) if flip else part
                    out_ref = send_ref if place >= 2 else keep_ref
                    out_ref[pl.ds((place & 1) * quarter + step * group, group)] = product[
                        slot, :, :, first : first + width
                    ].astype(out_ref.dtype)
            return carry

        if group == quarter:
            body(0, 0)
        else:
            lax.fori_loop(0, quarter // group, body, 0)


def chunk_shapes(chunks, count, block):
    return [
        jax.ShapeDtypeStruct((count // 2, block, width), kind)
        for _, width, _ in chunks
        for kind in (BF16, F32)
    ]


def own_kernel(bits, block, chunks, x_hbm, head_hbm, in_hbm, out_hbm, gain_in_ref, gain_out_ref, *refs):
    outs, scaled_ref = refs[: 2 * len(chunks)], refs[2 * len(chunks)]
    x_ref, head_ref, small_ref, table_ref, sems = refs[2 * len(chunks) + 1 :]
    here = lax.axis_index("seq")
    columns = x_ref.shape[1]
    rank = in_hbm.shape[0]
    mine = pl.ds(pl.multiple_of(here * columns, LANES), columns)
    copies = [
        pltpu.make_async_copy(head_hbm.at[:, mine], head_ref, sems.at[0]),
        pltpu.make_async_copy(in_hbm.at[:, mine], small_ref.at[:rank], sems.at[1]),
        pltpu.make_async_copy(out_hbm.at[:, mine], small_ref.at[rank:], sems.at[2]),
        pltpu.make_async_copy(x_hbm, x_ref, sems.at[3]),
    ]
    for copy in copies:
        copy.start()
    gain_in = gain_row(gain_in_ref, mine)
    gain_both = gain_in * gain_row(gain_out_ref, mine)
    copies[0].wait()
    scaled_ref[...] = (head_ref[...].astype(F32) * gain_both).astype(BF16)
    table_ref[2 * rank :, :] = scaled_ref[...]
    copies[1].wait()
    copies[2].wait()
    table_ref[: 2 * rank, :] = (small_ref[...].astype(F32) * gain_in).astype(BF16)
    copies[3].wait()
    pairs = list(zip(outs[0::2], outs[1::2]))
    block_products(here, bits, block, chunks, x_ref, table_ref, pairs)


def own_products(x, head, w_in, w_out, in_row, out_row, chunks, count, block):
    bits = count.bit_length() - 1
    columns = x.shape[1]
    width = sum(chunk[1] for chunk in chunks)
    shapes = chunk_shapes(chunks, count, block)
    shapes.append(jax.ShapeDtypeStruct((head.shape[0], columns), BF16))
    return pl.pallas_call(
        functools.partial(own_kernel, bits, block, chunks),
        in_specs=[ANY] * 4 + [VMEM] * 2,
        out_specs=[VMEM] * len(shapes),
        out_shape=shapes,
        scratch_shapes=[
            pltpu.VMEM(x.shape, BF16),
            pltpu.VMEM((head.shape[0], columns), BF16),
            pltpu.VMEM((2 * w_in.shape[0], columns), BF16),
            pltpu.VMEM((width, columns), BF16),
            pltpu.SemaphoreType.DMA((4,)),
        ],
        cost_estimate=pl.CostEstimate(
            flops=2 * x.shape[0] * columns * width,
            bytes_accessed=2 * x.shape[0] * columns + 2 * width * columns,
            transcendentals=0,
        ),
        name="own_products",
    )(x, head, w_in, w_out, in_row, out_row)


def far_kernel(bits, block, chunks, x_ref, table_ref, *outs):
    outs, zero_ref = outs[:-1], outs[-1]
    zero_ref[...] = jnp.zeros(zero_ref.shape, F32)
    pairs = list(zip(outs[0::2], outs[1::2]))
    block_products(lax.axis_index("seq"), bits, block, chunks, x_ref, table_ref, pairs)


def far_products(x, table, chunks, count, block):
    bits = count.bit_length() - 1
    shapes = chunk_shapes(chunks, count, block)
    shapes.append(jax.ShapeDtypeStruct((1, LANES), F32))
    return pl.pallas_call(
        functools.partial(far_kernel, bits, block, chunks),
        in_specs=[VMEM] * 2,
        out_specs=[VMEM] * len(shapes),
        out_shape=shapes,
        cost_estimate=pl.CostEstimate(
            flops=2 * x.shape[0] * x.shape[1] * table.shape[0],
            bytes_accessed=2 * x.shape[0] * x.shape[1] + 2 * table.shape[0] * x.shape[1],
            transcendentals=0,
        ),
        name="far_products",
    )(x, table)


def owner_kernel(depth, slots, chunks, *refs):
    keeps, gots = refs[:chunks], refs[chunks : 2 * chunks]
    stats_ref, marks_ref, turn_ref, own_t_ref, far_t_ref, own_h_ref, far_h_ref, gram_ref = refs[
        2 * chunks : 2 * chunks + 8
    ]
    factor_ref, table_ref, away_ref, gram_out_ref = refs[2 * chunks + 8 :]
    sums = [None] * chunks
    for slot, keep, got in zip(slots, keeps, gots):
        sums[slot] = keep[0] + got[0].astype(F32)
    rank2 = LANES
    rank = rank2 // 2
    half = rank // 2
    raw_latent = sums[0][:, :rank]
    raw_cross = sums[0][:, rank:rank2]
    raw_logits = jnp.concatenate([sums[0][:, rank2:]] + sums[1:], axis=1)
    inverse_in = lax.rsqrt(stats_ref[:, 0:1] * (1.0 / depth) + EPSILON)
    latent = raw_latent * inverse_in
    cosine = turn_ref[:, :rank]
    sine = turn_ref[:, rank:rank2]

    def swapped(value):
        return jnp.concatenate([value[:, half:], value[:, :half]], axis=1)

    turned = latent * cosine + swapped(latent) * sine
    sigmoid = 1.0 / (1.0 + jnp.exp(-turned))
    active = (turned * sigmoid).astype(BF16)
    active_wide = active.astype(F32)
    gram_part = mm(active, gram_ref[...].astype(BF16), 1, 0)
    cross = raw_cross * inverse_in
    square = (
        inverse_in * inverse_in * stats_ref[:, 1:2]
        + jnp.sum(active_wide * (2.0 * cross + gram_part), axis=1, keepdims=True)
    )
    inverse_out = lax.rsqrt(jnp.maximum(square, 0.0) * (1.0 / depth) + EPSILON)
    head_out = jnp.concatenate([own_h_ref[...], far_h_ref[...]], axis=1)
    head_high = head_out.astype(BF16)
    head_low = (head_out - head_high.astype(F32)).astype(BF16)
    logits = inverse_out * (
        raw_logits * inverse_in + (mm(active, head_high, 1, 0) + mm(active, head_low, 1, 0))
    )
    teacher = jnp.concatenate([own_t_ref[...], far_t_ref[...]], axis=1).astype(F32)
    student_top = jnp.max(logits, axis=1, keepdims=True)
    student = jnp.exp(logits - student_top)
    student_total = jnp.sum(student, axis=1, keepdims=True)
    student_lse = student_top + jnp.log(student_total)
    teacher_top = jnp.max(teacher, axis=1, keepdims=True)
    weight = jnp.exp(teacher - teacher_top)
    teacher_total = jnp.sum(weight, axis=1, keepdims=True)
    teacher_lse = teacher_top + jnp.log(teacher_total)
    prob_teacher = weight * (1.0 / teacher_total)
    prob_student = student * (1.0 / student_total)
    hits = lax.broadcasted_iota(jnp.int32, logits.shape, 1) == marks_ref[:, 0:1]
    picked = jnp.sum(jnp.where(hits, logits, 0.0), axis=1, keepdims=True)
    mask = marks_ref[:, 1:2].astype(F32)
    overlap = jnp.sum(prob_teacher * (teacher - logits), axis=1, keepdims=True)
    loss = mask * (overlap - teacher_lse + student_lse + HARD_WEIGHT * (student_lse - picked))
    grad_logits = (
        mask
        * (
            prob_student
            - prob_teacher
            + HARD_WEIGHT * (prob_student - jnp.where(hits, 1.0, 0.0))
        )
    ).astype(BF16)
    mean = jnp.sum(grad_logits.astype(F32) * logits, axis=1, keepdims=True) * (1.0 / depth)
    through = mm(grad_logits, head_high, 1, 1) + mm(grad_logits, head_low, 1, 1)
    grad_active = inverse_out * (through - mean * inverse_out * (cross + gram_part))
    grad_turned = grad_active * sigmoid * (1.0 + turned * (1.0 - sigmoid))
    grad_latent = grad_turned * cosine - swapped(grad_turned) * sine
    weight_back = -inverse_out * inverse_out * mean
    factor_ref[...] = jnp.concatenate(
        [inverse_in * grad_latent, (inverse_in * weight_back) * active_wide], axis=1
    ).astype(BF16)
    table = mm((inverse_out * active_wide).astype(BF16), grad_logits, 0, 0)
    slice_width = own_h_ref.shape[1]
    parts = slice_width // LANES
    for part in range(parts):
        table_ref[part * rank : (part + 1) * rank, :] = table[:, part * LANES : (part + 1) * LANES]
        away_ref[part * rank : (part + 1) * rank, :] = table[
            :, slice_width + part * LANES : slice_width + (part + 1) * LANES
        ]
    lines = jnp.broadcast_to(loss, (loss.shape[0], LANES)).T[:8]
    table_ref[parts * rank :, :] = lines
    away_ref[parts * rank :, :] = lines
    own_gram = mm((weight_back * active_wide).astype(BF16), active, 0, 0)
    gram_out_ref[...] = jnp.concatenate([own_gram[:half], own_gram[half:]], axis=1).astype(BF16)


def owner_step(depth, rank, slots, keeps, gots, stats, marks, turn, teachers, heads, gram):
    block = stats.shape[0]
    rows = heads[0].shape[1] // LANES * rank + 8
    operands = [*keeps, *gots, stats, marks, turn, *teachers, *heads, gram]
    return pl.pallas_call(
        functools.partial(owner_kernel, depth, slots, len(keeps)),
        in_specs=[VMEM] * len(operands),
        out_specs=[VMEM] * 4,
        out_shape=[
            jax.ShapeDtypeStruct((block, 2 * rank), BF16),
            jax.ShapeDtypeStruct((rows, block), F32),
            jax.ShapeDtypeStruct((rows, block), F32),
            jax.ShapeDtypeStruct((rank // 2, 2 * rank), BF16),
        ],
        name="owner",
    )(*operands)


def first_payload_kernel(factor_ref, table_ref, got_ref, gram_ref, out_ref):
    block = factor_ref.shape[0]
    rows = table_ref.shape[0] - 8
    out_ref[:block, :] = factor_ref[...]
    out_ref[block : block + rows, :] = (table_ref[:rows, :] + got_ref[:rows, :]).astype(BF16)
    out_ref[block + rows :, :] = gram_ref[...]


def next_payload_kernel(split, mine_ref, got_ref, out_ref):
    out_ref[:split, :] = mine_ref[:split, :]
    out_ref[split : 2 * split, :] = got_ref[:split, :]
    out_ref[2 * split :, :] = (
        mine_ref[split:, :].astype(F32) + got_ref[split:, :].astype(F32)
    ).astype(BF16)


def joined(kernel, rows, *operands):
    return pl.pallas_call(
        kernel,
        in_specs=[VMEM] * len(operands),
        out_specs=VMEM,
        out_shape=jax.ShapeDtypeStruct((rows, LANES), BF16),
        name="joined",
    )(*operands)


def final_kernel(bits, block, rank, x_ref, head_hbm, out_hbm, gain_in_ref, gain_out_ref, mine_ref,
                 got_ref, near_ref, away_ref, turned_ref, head_ref, small_ref, order_ref, sems):
    here = lax.axis_index("seq")
    columns = x_ref.shape[1]
    mine = pl.ds(pl.multiple_of(here * columns, LANES), columns)
    copies = [
        pltpu.make_async_copy(head_hbm.at[:, mine], head_ref, sems.at[0]),
        pltpu.make_async_copy(out_hbm.at[:, mine], small_ref, sems.at[1]),
    ]
    for copy in copies:
        copy.start()
    half = 1 << (bits - 1)
    for base, source in ((0, mine_ref), (half, got_ref)):

        def body(place, carry, base=base, source=source):
            owner = mirrored(base + place, bits) ^ here
            order_ref[pl.ds(pl.multiple_of(owner * block, block), block), :] = source[
                pl.ds(pl.multiple_of(place * block, block), block), :
            ]
            return carry

        if half <= 8:
            for place in range(half):
                body(place, 0)
        else:
            lax.fori_loop(0, half, body, 0)
    parts = head_ref.shape[0] // LANES
    rows = half * block
    summed = mine_ref[rows:, :].astype(F32) + got_ref[rows:, :].astype(F32)
    table = jnp.concatenate(
        [summed[part * rank : (part + 1) * rank, :] for part in range(parts)], axis=1
    ).astype(BF16)
    packed = summed[parts * rank :, :]
    gram = jnp.concatenate([packed[:, :rank], packed[:, rank:]], axis=0).astype(BF16)
    from_x = mm(order_ref[...], x_ref[...], 0, 0) * gain_row(gain_in_ref, mine)
    for copy in copies:
        copy.wait()
    from_head = mm(table, head_ref[...], 1, 0) * gain_row(gain_out_ref, mine)
    from_out = mm(gram, small_ref[...], 1, 0)
    total = jnp.concatenate([from_x[:rank], from_x[rank:] + from_head + from_out], axis=0)
    turned_ref[...] = total.T
    rows = columns // 2
    core = lax.axis_index("vocab")
    near_ref[...] = turned_ref[pl.ds(pl.multiple_of(core * rows, 8), rows), :]
    away_ref[...] = turned_ref[pl.ds(pl.multiple_of((1 - core) * rows, 8), rows), :]


def final_step(x, head, w_out, in_row, out_row, mine, got, count, block):
    bits = count.bit_length() - 1
    columns = x.shape[1]
    rank = w_out.shape[0]
    return pl.pallas_call(
        functools.partial(final_kernel, bits, block, rank),
        in_specs=[VMEM, ANY, ANY, VMEM, VMEM, VMEM, VMEM],
        out_specs=[VMEM] * 2,
        out_shape=[jax.ShapeDtypeStruct((columns // 2, 2 * rank), F32)] * 2,
        scratch_shapes=[
            pltpu.VMEM((columns, 2 * rank), F32),
            pltpu.VMEM((head.shape[0], columns), BF16),
            pltpu.VMEM((rank, columns), BF16),
            pltpu.VMEM((x.shape[0], 2 * rank), BF16),
            pltpu.SemaphoreType.DMA((2,)),
        ],
        name="final",
    )(x, head, w_out, in_row, out_row, mine, got)


def on_device(
    features, positions, token_ids, valid, teacher_logits, in_gain, final_gain, w_in, w_out, head
):
    count = lax.axis_size("seq")
    bits = count.bit_length() - 1
    here = lax.axis_index("seq")
    core = lax.axis_index("vocab")
    x = features[0]
    block = x.shape[0] // count
    columns = x.shape[1]
    rank, depth = w_in.shape
    half = rank // 2
    slice_width = head.shape[0]
    vocabulary = 2 * slice_width
    in_row, out_row = in_gain, final_gain
    if columns % (2 * LANES):
        in_row, out_row = in_gain.reshape(1, depth), final_gain.reshape(1, depth)

    width = 2 * rank + slice_width
    early = [(0, width - 256, False), (width - 256, 256, True)]
    late = [(0, slice_width // 2, False), (slice_width // 2, slice_width // 2, False)]
    made = own_products(x, head, w_in, w_out, in_row, out_row, early, count, block)
    far_table = swap_cores(made[-1])
    more = far_products(x, far_table, late, count, block)
    sends = [made[0], made[2], more[0], more[2]]
    keeps = [made[1], made[3], more[1], more[3]]
    flips = [chunk[2] for chunk in early + late]

    x_late, late_args, more = lax.optimization_barrier(
        (x, (positions, token_ids, valid, teacher_logits, in_gain, final_gain, w_out, head), more)
    )
    positions, token_ids, valid, teacher_logits, in_gain, final_gain, w_late, head_late = late_args
    in_wide, final_wide = in_gain.astype(F32), final_gain.astype(F32)
    squares = jnp.square(x_late.astype(F32))
    in_columns = lax.dynamic_slice_in_dim(in_wide, here * columns, columns, axis=0)
    sums = jnp.stack([jnp.sum(squares, axis=1), jnp.sum(squares * jnp.square(in_columns), axis=1)])
    order = jnp.array([mirrored(place, bits) for place in range(count)], jnp.int32) ^ here
    stats = jnp.take(sums.reshape(2, count, block), order, axis=1)
    own_teacher = lax.dynamic_index_in_dim(teacher_logits, core, 0, keepdims=False)
    far_teacher = swap_cores(lax.dynamic_index_in_dim(teacher_logits, 1 - core, 0, keepdims=False))

    scaled_out = (w_late.astype(F32) * final_wide).astype(BF16)
    own_out = mm(scaled_out, head_late, 1, 1)
    far_out = swap_cores(own_out)
    gram = mm(w_late, w_late, 1, 1)

    freqs = jnp.exp(-math.log(ROPE_BASE) * jnp.arange(half, dtype=F32) / half)
    angles = positions[0].astype(F32)[:, None] * freqs[None, :]
    cosine, sine = jnp.cos(angles), jnp.sin(angles)
    turn = jnp.concatenate([cosine, cosine, -sine, sine], axis=1)
    labels = lax.dynamic_index_in_dim(token_ids, core, 0, keepdims=False)
    labels = lax.rem(labels + core * slice_width, vocabulary)
    marks = jnp.stack([labels, lax.dynamic_index_in_dim(valid, core, 0, keepdims=False)], axis=1)

    for step in range(bits):
        gots = [
            swap_with(send, (1 << (1 - step if flip and step < 2 else step)), count)
            for send, flip in zip(sends, flips)
        ]
        left = count >> (step + 1)
        stats = stats[:, :left] + swap_with(stats[:, left:], 1 << step, count)
        if step == bits - 1:
            break
        keeps = [keep[:left] + got.astype(F32) for keep, got in zip(keeps, gots)]
        if step == 0:
            for index, (_, wide, _) in enumerate(early):
                keeps[index] = keeps[index] + jnp.broadcast_to(more[-1][0, 0], keeps[index].shape)
        sends = [value[left // 2 :].astype(BF16) for value in keeps]

    factor, table, away, gram_out = owner_step(
        depth, rank, (0, 1, 2, 3), keeps, gots, stats[:, 0].T, marks, turn,
        (own_teacher, far_teacher), (own_out, far_out), gram,
    )
    got = swap_cores(away)
    rows = table.shape[0] - 8
    payload = joined(
        first_payload_kernel, block + rows + rank // 2, factor, table, got, gram_out
    )
    own_loss, far_loss = table[rows : rows + 1], got[rows : rows + 1]
    row_loss = jnp.where(
        core == 0,
        jnp.concatenate([own_loss, far_loss]),
        jnp.concatenate([far_loss, own_loss]),
    )
    split = block
    for step in reversed(range(bits)):
        got = swap_with(payload, 1 << step, count)
        if step:
            kernel = functools.partial(next_payload_kernel, split)
            payload = joined(kernel, payload.shape[0] + split, payload, got)
            split *= 2
            if step == 1:
                payload, row_loss = lax.optimization_barrier((payload, row_loss))

    near, away = final_step(x, head, w_out, in_row, out_row, payload, got, count, block)
    return (near + swap_cores(away), row_loss)


def solution(mesh):
    placed = (
        P("vocab", "groups", "seq"),
        P("vocab", ("groups", "seq")),
        P(None, ("groups", "seq")),
        P(None, ("groups", "seq")),
        P(None, ("groups", "seq"), "vocab"),
        P(),
        P(),
        P(),
        P(),
        P("vocab", None),
    )
    return jax.shard_map(
        on_device,
        mesh=mesh,
        in_specs=placed,
        out_specs=(P(("groups", "seq", "vocab"), None), P(None, ("groups", "seq"))),
        check_vma=False,
    )
```
